32 devices in a mesh: dp: 16 (over z, y, x), mp: 2 (over core).
Axes of the slice: x: 2, y: 2, z: 4, core: 2. Of those that a mesh axis runs over, the one named last changes fastest.
Arguments:
- images: bfloat16 [32768, 384], P('dp'), may hold values from -6 to 6
- means: float32 [8192, 384], P(('mp', 'dp')), may hold values from -0.6 to 0.6
- precisions: float32 [8192, 384], P(('mp', 'dp')), may hold values from 0.5 to 2
- logits: float32 [8192], replicated, may hold values from -6 to 6
Outputs:
- new_means: float32 [8192, 384], P(('mp', 'dp'))
- new_variances: float32 [8192, 384], P(('mp', 'dp'))
- new_log_weights: float32 [8192], P(('mp', 'dp'))
- log_likelihood: float32 [32768], P('dp')
The draws below stay inside these ranges and needn't reach their ends.
All inputs are finite; a program needn't handle non-finite values.
Results may differ from the reference program's by a relative error of at most 0.0039.
The reference program's roundings to bfloat16 on the way (of `squares`, `prec_b`, `scaled` and `shares`) count: a program that leaves them out, or rounds other values in their place, can miss the bound.
Values may be sent and summed in bfloat16 or wider, within the bound.
A program may use at most 128 MiB of HBM per device.

```python
import math
import jax
import jax.numpy as jnp
from jax import lax

D = 384
K = 8192
TOK_DEV = 2048
N = 32768
N_DP = 16


def block_levels(key, extent, shards, least, largest):
    loudness = 1.0
    for dim, parts in shards:
        steps = jax.random.uniform(jax.random.fold_in(jax.random.fold_in(key, 6), dim), (parts,), jnp.float32, least / len(shards), largest / len(shards))
        loudness = loudness * jnp.repeat(jnp.exp(steps), extent[dim] // parts).reshape((-1,) + (1,) * (len(extent) - 1 - dim))
    return loudness


def noise(rng, extent, scale, reach, cuts=(), dtype=jnp.bfloat16):
    array = jax.random.normal(rng, extent, jnp.float32) * scale
    if len(cuts) > 0:
        array = block_levels(rng, extent, cuts, -0.22, 0.18) * array
    return jnp.clip(array, min=-reach, max=reach).astype(dtype)


def setup_inputs(seed: int = 0) -> dict:
    key_list = jax.random.split(jax.random.key(seed), 5)
    return {
        "images": noise(key_list[0], (N, D), 1.0, 6.0, ((0, 16),)),
        "means": noise(key_list[1], (K, D), 0.1, 0.6, ((0, 32),), jnp.float32),
        "precisions": jnp.clip(jnp.exp(math.log(2.0) - 1.3862944 * jax.random.uniform(key_list[2], (K, D), jnp.float32) ** block_levels(key_list[2], (K, D), ((0, 32),), -0.2, 0.2)), 0.5, 2.0),
        "logits": noise(key_list[3], (K,), 1.0, 6.0, (), jnp.float32),
    }


def matmul_t(left, right):
    return jnp.dot(left.astype(jnp.float32), right.astype(jnp.float32).T, preferred_element_type=jnp.float32, precision=lax.Precision.HIGHEST)


def reference(images, means, precisions, logits):
    prec_b = precisions.astype(jnp.bfloat16)
    scaled = (means * precisions).astype(jnp.bfloat16)
    offset = logits + 0.5 * jnp.sum(jnp.log(precisions) - means * means * precisions, axis=1) - 0.5 * D * math.log(2.0 * math.pi)
    logit_peak = jnp.max(logits)
    logit_total = logit_peak + jnp.log(jnp.sum(jnp.exp(logits - logit_peak)))
    blocks = images.reshape(N_DP, TOK_DEV, D)

    def update(running, image_block):
        counts, moments = running
        squares = (image_block.astype(jnp.float32) * image_block.astype(jnp.float32)).astype(jnp.bfloat16)
        scores = -0.5 * matmul_t(squares, prec_b) + matmul_t(image_block, scaled) + offset[None, :]
        row_peak = jnp.max(scores, axis=1)
        row_total = row_peak + jnp.log(jnp.sum(jnp.exp(scores - row_peak[:, None]), axis=1))
        shares = jnp.exp(scores - row_total[:, None]).astype(jnp.bfloat16)
        features = jnp.concatenate([image_block, squares], axis=1)
        counts = counts + jnp.sum(shares.astype(jnp.float32), axis=0)
        moments = moments + jnp.dot(shares.astype(jnp.float32).T, features.astype(jnp.float32), preferred_element_type=jnp.float32, precision=lax.Precision.HIGHEST)
        return (counts, moments), row_total - logit_total

    start = (jnp.zeros((K,), jnp.float32), jnp.zeros((K, 2 * D), jnp.float32))
    (counts, moments), likely = lax.scan(update, start, blocks)
    denominator = counts + 1.0
    new_means = (moments[:, :D] + means) / denominator[:, None]
    second = (moments[:, D:] + 1.0 / precisions + means * means) / denominator[:, None]
    new_variances = second - new_means * new_means
    new_log_weights = jnp.log(denominator) - jnp.log(jnp.float32(N + K))
    return new_means, new_variances, new_log_weights, likely.reshape(-1)
```

```python
import functools
import math

import jax
import jax.numpy as jnp
from jax import lax
from jax.experimental import pallas as pl
from jax.experimental.pallas import tpu as pltpu
from jax.sharding import Mesh, PartitionSpec as P

MESH = pl.DeviceIdType.MESH
SQUARE = 4
PIECES = 2
TILES = 2
F32 = jnp.float32
BF16 = jnp.bfloat16
VMEM_LIMIT = 67_043_328


def remote(src, dst, send, recv, device):
    return pltpu.make_async_remote_copy(
        src_ref=src, dst_ref=dst, send_sem=send, recv_sem=recv, device_id=device, device_id_type=MESH
    )


def target(k, a, n):
    left, right = a, n - 1 - a
    far, near = jnp.maximum(left, right), jnp.minimum(left, right)
    lead = far - near
    late = jnp.maximum(k - lead, 0)
    dist = jnp.where(k < lead, far - k, near - late // 2)
    to_far = jnp.logical_or(k < lead, lax.rem(late, 2) == 1)
    to_right = jnp.where(right >= left, to_far, jnp.logical_not(to_far))
    return jnp.where(to_right, a + dist, a - dist)


def schedule(n_ca):
    b, c = n_ca - 2, n_ca - 1
    both, near, far, early, late = (0, 4), (1, 1), (5, 1), (0, 1), (4, 1)
    shapes = (
        (0, 1, both, 2),
        (1, b, both, 2),
        (0, b, near, 2),
        (b, c, both, 2),
        (b, c, near, 2),
        (0, c, far, 2),
        (0, c, (3, 1), 1),
        (c, n_ca, early, 4),
        (0, c, (7, 1), 1),
        (c, n_ca, late, 4),
    )
    out, t = [], 0
    for q0, q1, (p0, stride), count in shapes:
        out.append((t, q0, p0, stride, count))
        t += (q1 - q0) * count
    return out, t


def em_kernel(n_ca, n_mp, halves, img_ref, means_ref, prec_ref, logits_ref,
              first_ref, second_ref, den_ref, like_ref,
              feats, wall, offall, ebuf, peak, blk_lse, lse, tot, lbuf, acc, cacc, crow, sbuf, sc, rbuf, rc,
              loc, isend, irecv, wsend, wrecv, osend, orecv, lsend, lrecv, msend, mrecv, csend, crecv):
    a, b, m = lax.axis_index("ca"), lax.axis_index("ib"), lax.axis_index("mp")
    t_rows, d = img_ref.shape
    r = means_ref.shape[0]
    rh = r // halves
    core = lax.rem(m, 2)
    partner = m + 1 - 2 * core
    bx = b + 1 - 2 * lax.rem(b, 2)
    by = lax.rem(b + 2, 4)
    bd = lax.rem(bx + 2, 4)
    to_x, to_y, to_p = (a, bx, m), (a, by, m), (a, b, partner)
    sub = t_rows // (2 * PIECES)
    part_rows = 2 * sub
    n = SQUARE * n_mp
    me = b * n_mp + m

    def peer(k):
        p = lax.rem(me + k, n)
        return (a, p // n_mp, lax.rem(p, n_mp))

    barrier = pltpu.get_barrier_semaphore()

    @pl.loop(1, n)
    def _(k):
        pl.semaphore_signal(barrier, inc=1, device_id=peer(k), device_id_type=MESH)

    @pl.when(a > 0)
    def _():
        pl.semaphore_signal(barrier, inc=1, device_id=(a - 1, b, m), device_id_type=MESH)

    @pl.when(a < n_ca - 1)
    def _():
        pl.semaphore_signal(barrier, inc=1, device_id=(a + 1, b, m), device_id_type=MESH)

    def image_cols(i, rows):
        return feats.at[i, rows, pl.ds(d, d)]

    own = pltpu.make_async_copy(img_ref, feats.at[b, :, pl.ds(d, d)], loc.at[0])
    own.start()

    means, prec = means_ref[...], prec_ref[...]
    wall[a] = jnp.concatenate([-0.5 * prec.astype(BF16), (means * prec).astype(BF16)], axis=1)
    terms = 0.5 * jnp.sum(jnp.log(prec) - means * means * prec, axis=1, keepdims=True)
    row = jnp.broadcast_to(terms, (r, 128)).T[:1]
    offall[a] = logits_ref[(m * n_ca + a) * SQUARE + b] + row - 0.5 * d * math.log(2.0 * math.pi)

    ends = (a == 0).astype(jnp.int32) + (a == n_ca - 1).astype(jnp.int32)
    pl.semaphore_wait(barrier, n + 1 - ends)

    def img_copy(k, i, dev, piece, first=False):
        rows = pl.ds(pl.multiple_of((piece * 2 + core) * sub, sub), sub)
        dst = image_cols(i, rows)
        return remote(img_ref.at[rows] if first else dst, dst, isend.at[k, piece], irecv.at[k, piece], dev)

    def has_next(way):
        return a < n_ca - 1 if way == 0 else a > 0

    def hop(way, dist, sender):
        blk = jnp.clip(sender - dist + 2 * way * dist, 0, n_ca - 1)
        return blk, (jnp.clip(a + 1 - 2 * way, 0, n_ca - 1), b, m)

    def w_copy(way, dist, h, sender):
        blk, dev = hop(way, dist, sender)
        block = wall.at[blk, pl.ds(h * rh, rh)]
        return remote(block, block, wsend.at[way, dist, h], wrecv.at[way, dist, h], dev)

    def off_copy(way, dist, sender):
        blk, dev = hop(way, dist, sender)
        return remote(offall.at[blk], offall.at[blk], osend.at[way, dist], orecv.at[way, dist], dev)

    def exists(way, dist):
        blk = a - dist + 2 * way * dist
        return jnp.logical_and(blk >= 0, blk < n_ca)

    def forward(way, dist, h):
        @pl.when(has_next(way))
        def _():
            w_copy(way, dist, h, a).start()
            if h == 0:
                off_copy(way, dist, a).start()

    for piece in range(PIECES):
        img_copy(0, b, to_x, piece, True).start()
        img_copy(1, b, to_y, piece, True).start()
    for h in range(halves):
        for way in (0, 1):
            forward(way, 0, h)

    def event(u):
        dist, h = u // halves + 1, u % halves
        for way in (0, 1):
            @pl.when(exists(way, dist))
            def _():
                sender = a - 1 + 2 * way
                w_copy(way, dist - 1, h, sender).wait_recv()
                if h == 0:
                    off_copy(way, dist - 1, sender).wait_recv()
                if dist < n_ca - 1:
                    forward(way, dist, h)

    def images_in(piece):
        img_copy(0, bx, to_x, piece).wait_recv()
        img_copy(3, bx, to_p, piece).start()

        @pl.when(core == 0)
        def _():
            img_copy(2, bx, to_y, piece).start()

        img_copy(1, by, to_y, piece).wait_recv()
        img_copy(4, by, to_p, piece).start()

        @pl.when(core == 1)
        def _():
            img_copy(2, by, to_x, piece).start()

    def corner_in(piece):
        img_copy(2, bd, to_x, piece).wait_recv()
        img_copy(5, bd, to_p, piece).start()

    def square(i, piece):
        rows = pl.ds(pl.multiple_of(piece * part_rows, part_rows), part_rows)
        wide = feats[i, rows, d:].astype(F32)
        feats[i, rows, :d] = (wide * wide).astype(BF16)

    def paired(k, i, piece):
        img_copy(k, i, to_p, piece).wait_recv()
        square(i, piece)

    own.wait()
    for piece in range(PIECES):
        square(b, piece)

    def shard(p):
        return jnp.where(p == 0, b, jnp.where(p == 1, bx, jnp.where(p == 2, by, bd)))

    def send_lse(k, hh):
        return remote(lse.at[hh], lbuf.at[k, hh], lsend.at[k, hh], lrecv.at[k, hh], peer(k))

    def reduce_lse(hh):
        high = lax.fori_loop(1, n_ca, lambda k, h: jnp.maximum(h, blk_lse[k, hh]), blk_lse[0, hh])
        tot = lax.fori_loop(
            1, n_ca, lambda k, x: x + jnp.exp(blk_lse[k, hh] - high), jnp.exp(blk_lse[0, hh] - high)
        )
        lse[hh] = high + jnp.log(tot)

    def share_lse(hh):
        @pl.loop(1, n)
        def _(k):
            send_lse(k, hh).start()

    rects, tiles = schedule(n_ca)
    pair = [x[0] // TILES for x in rects]
    events = (n_ca - 1) * halves

    def tile(t):
        q, part = t, t
        for t0, q0, p0, stride, count in rects:
            here = t >= t0
            s = jnp.maximum(t - t0, 0)
            q = jnp.where(here, q0 + s // count, q)
            part = jnp.where(here, p0 + stride * lax.rem(s, count), part)
        j = target(n_ca - 1 - q, a, n_ca)
        hh = part // SQUARE
        i = shard(part - SQUARE * hh)
        cols = pl.ds(pl.multiple_of(hh * part_rows, part_rows), part_rows)
        s = lax.dot_general(wall[j], feats[i, cols], (((1,), (1,)), ((), ())), preferred_element_type=F32)
        column = jnp.broadcast_to(offall[j], (128, r)).T
        s = s + column[:, :1]
        top = jnp.max(s, axis=0, keepdims=True)
        e = jnp.exp(s - top)
        ebuf[j, i, :, cols] = e
        peak[j, hh, i] = top
        blk_lse[j, hh, i] = top + jnp.log(jnp.sum(e, axis=0, keepdims=True))

    @pl.loop(0, tiles // TILES)
    def _(u):
        @pl.when(u == pair[1])
        def _():
            for v in range((n_ca - 3) * halves):
                event(v)
            images_in(0)

        @pl.when(u == pair[2])
        def _():
            paired(3, bx, 0)
            paired(4, by, 0)

        @pl.when(u == pair[3])
        def _():
            for v in range((n_ca - 3) * halves, (n_ca - 2) * halves):
                event(v)
            images_in(1)

        @pl.when(u == pair[5])
        def _():
            paired(3, bx, 1)
            paired(4, by, 1)

        @pl.when(u == pair[6] - 1)
        def _():
            corner_in(0)

        @pl.when(u == pair[6])
        def _():
            paired(5, bd, 0)

        @pl.when(u == pair[7])
        def _():
            for v in range((n_ca - 2) * halves, events):
                event(v)

        @pl.when(u == pair[7] + 1)
        def _():
            corner_in(1)

        @pl.when(u == pair[8])
        def _():
            paired(5, bd, 1)

        @pl.when(u == pair[8] + 1)
        def _():
            reduce_lse(0)

        @pl.when(u == pair[8] + 2)
        def _():
            share_lse(0)

        for w in range(TILES):
            tile(TILES * u + w)

    reduce_lse(1)
    logits = logits_ref[...]
    top = jnp.max(jnp.max(logits, axis=0), axis=1, keepdims=True)
    logit_total = top + jnp.log(jnp.sum(jnp.sum(jnp.exp(logits - top[None]), axis=0), axis=1, keepdims=True))

    def finish_lse(hh):
        @pl.loop(1, n)
        def _(k):
            send_lse(k, hh).wait_recv()

        own_lse = lse[hh]
        high = lax.fori_loop(1, n, lambda k, h: jnp.maximum(h, lbuf[k, hh]), own_lse)
        total = lax.fori_loop(1, n, lambda k, x: x + jnp.exp(lbuf[k, hh] - high), jnp.exp(own_lse - high))
        row_total = high + jnp.log(total)
        tot[hh] = row_total
        like_ref[:, hh * part_rows:(hh + 1) * part_rows] = tot[hh, b] - logit_total

        @pl.loop(0, n_ca)
        def _(j):
            peak[j, hh] = jnp.exp(peak[j, hh] - row_total)

    share_lse(1)
    finish_lse(0)

    def info(k):
        j = target(k, a, n_ca)
        way = (j < a).astype(jnp.int32)
        joined = jnp.where(j < a, a < n_ca - 1, a > 0)
        return j, way, joined

    def slot(j, way, owner):
        return jnp.where(jnp.logical_and(j == owner, way == 1), n_ca, j)

    def out_copies(k, h):
        j, way, _ = info(k)
        nbr = jnp.clip(a + 1 - 2 * way, 0, n_ca - 1)
        dev = (nbr, b, m)
        s = slot(j, way, nbr)
        rows = pl.ds(pl.multiple_of(h * rh, rh), rh)
        return (
            remote(sbuf.at[j, rows], rbuf.at[s, rows], msend.at[j, h], mrecv.at[s, h], dev),
            remote(sc.at[j, h], rc.at[s, h], csend.at[j, h], crecv.at[s, h], dev),
        )

    def in_copies(j, way, h):
        nbr = jnp.clip(a - 1 + 2 * way, 0, n_ca - 1)
        dev = (nbr, b, m)
        s = slot(j, way, a)
        rows = pl.ds(pl.multiple_of(h * rh, rh), rh)
        return s, (
            remote(sbuf.at[j, rows], rbuf.at[s, rows], msend.at[j, h], mrecv.at[s, h], dev),
            remote(sc.at[j, h], rc.at[s, h], csend.at[j, h], crecv.at[s, h], dev),
        )

    def start_piece(v):
        for c in out_copies(v // halves, lax.rem(v, halves)):
            c.start()

    def merge(v):
        k, h = v // halves, lax.rem(v, halves)
        j, way, _ = info(k)
        s, copies = in_copies(j, way, h)
        for c in copies:
            c.wait_recv()
        rows = pl.ds(pl.multiple_of(h * rh, rh), rh)
        sbuf[j, rows] = (acc[k, rows] + rbuf[s, rows].astype(F32)).astype(BF16)
        sc[j, h] = crow[k, h] + rc[s, h]

    exports = (n_ca - 1) * halves

    def flush(v):
        @pl.when(jnp.logical_and(jnp.logical_and(v >= 1, v - 1 < exports), jnp.logical_not(info((v - 1) // halves)[2])))
        def _():
            start_piece(jnp.maximum(v - 1, 0))

        w = v - 1 - halves

        @pl.when(jnp.logical_and(w >= 0, info(jnp.maximum(w, 0) // halves)[2]))
        def _():
            start_piece(jnp.maximum(w, 0))

    def weigh(k, h, hh):
        j = target(k, a, n_ca)
        rows = pl.ds(pl.multiple_of(h * rh, rh), rh)
        cols = pl.ds(hh * part_rows, part_rows)
        prod = part = None
        for i in range(SQUARE):
            shares = (ebuf[j, i, rows, cols] * peak[j, hh, i]).astype(BF16)
            wide = shares.astype(F32)
            for q in range(part_rows // 128):
                lane = wide[:, q * 128:(q + 1) * 128]
                part = lane if part is None else part + lane
            p = jnp.dot(shares, feats[i, cols], preferred_element_type=F32)
            prod = p if prod is None else prod + p
        return prod, part

    def settle(v, k, h):
        rows = pl.ds(pl.multiple_of(h * rh, rh), rh)
        crow[k, h] = jnp.sum(cacc[...].T, axis=0, keepdims=True)

        @pl.when(jnp.logical_and(v < exports, jnp.logical_not(info(k)[2])))
        def _():
            j = info(k)[0]
            sbuf[j, rows] = acc[k, rows].astype(BF16)
            sc[j, h] = crow[k, h]

        w = v - halves

        @pl.when(jnp.logical_and(w >= 0, info(jnp.maximum(w, 0) // halves)[2]))
        def _():
            merge(jnp.maximum(w, 0))

    acc[0, :rh], cacc[...] = weigh(0, 0, 0)
    finish_lse(1)
    prod, part = weigh(0, 0, 1)
    acc[0, :rh] += prod
    cacc[...] += part
    settle(0, 0, 0)

    @pl.loop(1, n_ca * halves)
    def _(v):
        k, h = v // halves, lax.rem(v, halves)
        rows = pl.ds(pl.multiple_of(h * rh, rh), rh)
        prod, part = weigh(k, h, 0)
        acc[k, rows] = prod
        cacc[...] = part
        flush(v)
        prod, part = weigh(k, h, 1)
        acc[k, rows] += prod
        cacc[...] += part
        settle(v, k, h)

    first_ref[...] = acc[n_ca - 1, :, d:] + means_ref[...]
    second_ref[...] = acc[n_ca - 1, :, :d] + 1.0 / prec_ref[...] + means_ref[...] * means_ref[...]
    flush(n_ca * halves)

    def join(way, h):
        s, copies = in_copies(a, jnp.int32(way), h)
        for c in copies:
            c.wait_recv()
        rows = pl.ds(h * rh, rh)
        first_ref[rows] += rbuf[s, rows, d:].astype(F32)
        second_ref[rows] += rbuf[s, rows, :d].astype(F32)
        crow[n_ca - 1, h] += rc[s, h]

    for h in range(halves):
        @pl.when(a > 0)
        def _():
            join(0, h)

        @pl.when(a < n_ca - 1)
        def _():
            join(1, h)

    for h in range(halves):
        den_ref[h] = crow[n_ca - 1, h] + 1.0

    @pl.loop(0, exports)
    def _(v):
        for c in out_copies(v // halves, lax.rem(v, halves)):
            c.wait_send()

    for k, i in enumerate((b, b, bd, bx, by, bd)):
        for piece in range(PIECES):
            img_copy(k, i, to_p, piece).wait_send()

    for dist in range(n_ca - 1):
        for way in (0, 1):
            @pl.when(jnp.logical_and(exists(way, dist), has_next(way)))
            def _():
                for h in range(halves):
                    w_copy(way, dist, h, a).wait_send()
                off_copy(way, dist, a).wait_send()

    @pl.loop(1, n)
    def _(k):
        for hh in range(PIECES):
            send_lse(k, hh).wait_send()


def em(images, means, precisions, logits, n_ca, n_mp):
    t, d = images.shape
    r = means.shape[0]
    halves = 2 if r % 32 == 0 else 1
    n = SQUARE * n_mp
    vmem = pl.BlockSpec(memory_space=pltpu.VMEM)
    dma = pltpu.SemaphoreType.DMA
    line = dma((2, n_ca - 1, halves))
    short = dma((2, n_ca - 1))
    return pl.pallas_call(
        functools.partial(em_kernel, n_ca, n_mp, halves),
        out_shape=(
            jax.ShapeDtypeStruct((r, d), F32),
            jax.ShapeDtypeStruct((r, d), F32),
            jax.ShapeDtypeStruct((halves, 1, r // halves), F32),
            jax.ShapeDtypeStruct((1, t), F32),
        ),
        in_specs=[pl.BlockSpec(memory_space=pl.ANY), vmem, vmem, vmem],
        out_specs=(vmem,) * 4,
        scratch_shapes=[
            pltpu.VMEM((SQUARE, t, 2 * d), BF16),
            pltpu.VMEM((n_ca, r, 2 * d), BF16),
            pltpu.VMEM((n_ca, 1, r), F32),
            pltpu.VMEM((n_ca, SQUARE, r, t), F32),
            pltpu.VMEM((n_ca, PIECES, SQUARE, 1, t // PIECES), F32),
            pltpu.VMEM((n_ca, PIECES, SQUARE, 1, t // PIECES), F32),
            pltpu.VMEM((PIECES, SQUARE, 1, t // PIECES), F32),
            pltpu.VMEM((PIECES, SQUARE, 1, t // PIECES), F32),
            pltpu.VMEM((n, PIECES, SQUARE, 1, t // PIECES), F32),
            pltpu.VMEM((n_ca, r, 2 * d), F32),
            pltpu.VMEM((r // halves, 128), F32),
            pltpu.VMEM((n_ca, halves, 1, r // halves), F32),
            pltpu.VMEM((n_ca, r, 2 * d), BF16),
            pltpu.VMEM((n_ca, halves, 1, r // halves), F32),
            pltpu.VMEM((n_ca + 1, r, 2 * d), BF16),
            pltpu.VMEM((n_ca + 1, halves, 1, r // halves), F32),
            dma((1,)),
            dma((6, PIECES)),
            dma((6, PIECES)),
            line, line, short, short,
            dma((n, PIECES)),
            dma((n, PIECES)),
            dma((n_ca, halves)),
            dma((n_ca + 1, halves)),
            dma((n_ca, halves)),
            dma((n_ca + 1, halves)),
        ],
        compiler_params=pltpu.CompilerParams(
            collective_id=0, has_side_effects=True, vmem_limit_bytes=VMEM_LIMIT
        ),
        name="em",
    )(images, means, precisions, logits.reshape(-1, 1, r))


def body(n_ca, n_mp, images, means, precisions, logits):
    t, d = images.shape
    r = means.shape[0]
    first, second, denominator, like = em(images, means, precisions, logits, n_ca, n_mp)
    denominator = denominator.reshape(r)
    total = float(t * n_ca * SQUARE + logits.shape[0])
    new_means = first / denominator[:, None]
    new_variances = second / denominator[:, None] - new_means * new_means
    new_log_weights = jnp.log(denominator) - jnp.log(jnp.float32(total))
    return (new_means, new_variances, new_log_weights, like[0])


def solution(mesh):
    n_dp, n_mp = mesh.shape["dp"], mesh.shape["mp"]
    n_ca = n_dp // SQUARE
    split = Mesh(mesh.devices.reshape(n_ca, SQUARE, n_mp), ("ca", "ib", "mp"))
    dp = ("ca", "ib")
    comp = ("mp", "ca", "ib")
    return jax.shard_map(
        functools.partial(body, n_ca, n_mp),
        mesh=split,
        in_specs=(P(dp, None), P(comp, None), P(comp, None), P()),
        out_specs=(P(comp, None), P(comp, None), P(comp), P(dp)),
        check_vma=False,
    )
```

```python
import functools
import math

import jax
import jax.numpy as jnp
from jax import lax
from jax.experimental import pallas as pl
from jax.experimental.pallas import tpu as pltpu
from jax.sharding import Mesh, PartitionSpec as P

MESH = pl.DeviceIdType.MESH
SQUARE = 4
PIECES = 2
TILES = 2
F32 = jnp.float32
BF16 = jnp.bfloat16
VMEM_LIMIT = 67_043_328


def remote(src, dst, send, recv, device):
    return pltpu.make_async_remote_copy(
        src_ref=src, dst_ref=dst, send_sem=send, recv_sem=recv, device_id=device, device_id_type=MESH
    )


def target(k, a, n):
    left, right = a, n - 1 - a
    far, near = jnp.maximum(left, right), jnp.minimum(left, right)
    lead = far - near
    late = jnp.maximum(k - lead, 0)
    dist = jnp.where(k < lead, far - k, near - late // 2)
    to_far = jnp.logical_or(k < lead, lax.rem(late, 2) == 1)
    to_right = jnp.where(right >= left, to_far, jnp.logical_not(to_far))
    return jnp.where(to_right, a + dist, a - dist)


def schedule(n_ca):
    b, c = n_ca - 2, n_ca - 1
    both, near, far = (0, 4), (1, 1), (5, 1)
    shapes = (
        (0, 1, both, 2),
        (1, b, both, 2),
        (0, b, near, 2),
        (b, c, both, 2),
        (b, c, near, 2),
        (0, c, far, 2),
    )
    out, t = [], 0
    for q0, q1, (p0, stride), count in shapes:
        out.append((t, q0, p0, stride, count))
        t += (q1 - q0) * count
    return out, t


def em_kernel(n_ca, n_mp, halves, img_ref, means_ref, prec_ref, logits_ref,
              first_ref, second_ref, den_ref, like_ref,
              feats, wall, offall, offcol, ebuf, peak, blk_lse, lse, tot, lbuf, acc, cacc, crow, sbuf, sc, rbuf, rc,
              loc, isend, irecv, wsend, wrecv, osend, orecv, lsend, lrecv, msend, mrecv, csend, crecv):
    a, b, m = lax.axis_index("ca"), lax.axis_index("ib"), lax.axis_index("mp")
    t_rows, d = img_ref.shape
    r = means_ref.shape[0]
    rh = r // halves
    core = lax.rem(m, 2)
    partner = m + 1 - 2 * core
    bx = b + 1 - 2 * lax.rem(b, 2)
    by = lax.rem(b + 2, 4)
    bd = lax.rem(bx + 2, 4)
    to_x, to_y, to_p = (a, bx, m), (a, by, m), (a, b, partner)
    sub = t_rows // (2 * PIECES)
    part_rows = 2 * sub
    n = SQUARE * n_mp
    me = b * n_mp + m

    def peer(k):
        p = lax.rem(me + k, n)
        return (a, p // n_mp, lax.rem(p, n_mp))

    barrier = pltpu.get_barrier_semaphore()

    @pl.loop(1, n)
    def _(k):
        pl.semaphore_signal(barrier, inc=1, device_id=peer(k), device_id_type=MESH)

    @pl.when(a > 0)
    def _():
        pl.semaphore_signal(barrier, inc=1, device_id=(a - 1, b, m), device_id_type=MESH)

    @pl.when(a < n_ca - 1)
    def _():
        pl.semaphore_signal(barrier, inc=1, device_id=(a + 1, b, m), device_id_type=MESH)

    def image_cols(i, rows):
        return feats.at[i, rows, pl.ds(d, d)]

    own = pltpu.make_async_copy(img_ref, feats.at[b, :, pl.ds(d, d)], loc.at[0])
    own.start()

    means, prec = means_ref[...], prec_ref[...]
    wall[a] = jnp.concatenate([-0.5 * prec.astype(BF16), (means * prec).astype(BF16)], axis=1)
    terms = 0.5 * jnp.sum(jnp.log(prec) - means * means * prec, axis=1, keepdims=True)
    row = jnp.broadcast_to(terms, (r, 128)).T[:1]
    offall[a] = logits_ref[(m * n_ca + a) * SQUARE + b] + row - 0.5 * d * math.log(2.0 * math.pi)

    ends = (a == 0).astype(jnp.int32) + (a == n_ca - 1).astype(jnp.int32)
    pl.semaphore_wait(barrier, n + 1 - ends)

    def img_copy(k, i, dev, piece, first=False):
        rows = pl.ds(pl.multiple_of((piece * 2 + core) * sub, sub), sub)
        dst = image_cols(i, rows)
        return remote(img_ref.at[rows] if first else dst, dst, isend.at[k, piece], irecv.at[k, piece], dev)

    def has_next(way):
        return a < n_ca - 1 if way == 0 else a > 0

    def hop(way, dist, sender):
        blk = jnp.clip(sender - dist + 2 * way * dist, 0, n_ca - 1)
        return blk, (jnp.clip(a + 1 - 2 * way, 0, n_ca - 1), b, m)

    def w_copy(way, dist, h, sender):
        blk, dev = hop(way, dist, sender)
        block = wall.at[blk, pl.ds(h * rh, rh)]
        return remote(block, block, wsend.at[way, dist, h], wrecv.at[way, dist, h], dev)

    def off_copy(way, dist, sender):
        blk, dev = hop(way, dist, sender)
        return remote(offall.at[blk], offall.at[blk], osend.at[way, dist], orecv.at[way, dist], dev)

    def exists(way, dist):
        blk = a - dist + 2 * way * dist
        return jnp.logical_and(blk >= 0, blk < n_ca)

    def forward(way, dist, h):
        @pl.when(has_next(way))
        def _():
            w_copy(way, dist, h, a).start()
            if h == 0:
                off_copy(way, dist, a).start()

    for piece in range(PIECES):
        img_copy(0, b, to_x, piece, True).start()
        img_copy(1, b, to_y, piece, True).start()
    for h in range(halves):
        for way in (0, 1):
            forward(way, 0, h)

    def column(blk):
        offcol[blk] = jnp.broadcast_to(offall[blk], (128, r)).T

    def event(u):
        dist, h = u // halves + 1, u % halves
        for way in (0, 1):
            @pl.when(exists(way, dist))
            def _():
                sender = a - 1 + 2 * way
                w_copy(way, dist - 1, h, sender).wait_recv()
                if h == 0:
                    off_copy(way, dist - 1, sender).wait_recv()
                if dist < n_ca - 1:
                    forward(way, dist, h)
                if h == 0:
                    column(hop(way, dist - 1, sender)[0])

    def images_in(piece):
        img_copy(0, bx, to_x, piece).wait_recv()
        img_copy(3, bx, to_p, piece).start()

        @pl.when(core == 0)
        def _():
            img_copy(2, bx, to_y, piece).start()

        img_copy(1, by, to_y, piece).wait_recv()
        img_copy(4, by, to_p, piece).start()

        @pl.when(core == 1)
        def _():
            img_copy(2, by, to_x, piece).start()

    def corner_in(piece):
        img_copy(2, bd, to_x, piece).wait_recv()
        img_copy(5, bd, to_p, piece).start()

    def square(i, piece):
        rows = pl.ds(pl.multiple_of(piece * part_rows, part_rows), part_rows)
        wide = feats[i, rows, d:].astype(F32)
        feats[i, rows, :d] = (wide * wide).astype(BF16)

    def paired(k, i, piece):
        img_copy(k, i, to_p, piece).wait_recv()
        square(i, piece)

    own.wait()
    column(a)
    for piece in range(PIECES):
        square(b, piece)

    def shard(p):
        return jnp.where(p == 0, b, jnp.where(p == 1, bx, jnp.where(p == 2, by, bd)))

    def send_lse(k, hh):
        return remote(lse.at[hh], lbuf.at[k, hh], lsend.at[k, hh], lrecv.at[k, hh], peer(k))

    def reduce_lse(hh):
        high = lax.fori_loop(1, n_ca, lambda k, h: jnp.maximum(h, blk_lse[k, hh]), blk_lse[0, hh])
        tot = lax.fori_loop(
            1, n_ca, lambda k, x: x + jnp.exp(blk_lse[k, hh] - high), jnp.exp(blk_lse[0, hh] - high)
        )
        lse[hh] = high + jnp.log(tot)

    def share_lse(hh):
        @pl.loop(1, n)
        def _(k):
            send_lse(k, hh).start()

    rects, tiles = schedule(n_ca)
    pair = [x[0] // TILES for x in rects]
    events = (n_ca - 1) * halves

    def tile(q, p, hh):
        j = target(n_ca - 1 - q, a, n_ca)
        i = shard(p)
        cols = pl.ds(pl.multiple_of(hh * part_rows, part_rows), part_rows)
        s = lax.dot_general(wall[j], feats[i, cols], (((1,), (1,)), ((), ())), preferred_element_type=F32)
        s = s + offcol[j][:, :1]
        top = jnp.max(s, axis=0, keepdims=True)
        e = jnp.exp(s - top)
        ebuf[j, i, :, cols] = e
        peak[j, hh, i] = top
        blk_lse[j, hh, i] = top + jnp.log(jnp.sum(e, axis=0, keepdims=True))

    def early_tile(t):
        q, part = t, t
        for t0, q0, p0, stride, count in rects:
            here = t >= t0
            s = jnp.maximum(t - t0, 0)
            q = jnp.where(here, q0 + s // count, q)
            part = jnp.where(here, p0 + stride * lax.rem(s, count), part)
        hh = part // SQUARE
        tile(q, part - SQUARE * hh, hh)

    @pl.loop(0, tiles // TILES)
    def _(u):
        @pl.when(u == pair[1])
        def _():
            for v in range((n_ca - 3) * halves):
                event(v)
            images_in(0)

        @pl.when(u == pair[2])
        def _():
            paired(3, bx, 0)
            paired(4, by, 0)

        @pl.when(u == pair[3])
        def _():
            for v in range((n_ca - 3) * halves, (n_ca - 2) * halves):
                event(v)
            images_in(1)

        @pl.when(u == pair[5])
        def _():
            paired(3, bx, 1)
            paired(4, by, 1)

        @pl.when(u == tiles // TILES - 1)
        def _():
            corner_in(0)

        for w in range(TILES):
            early_tile(TILES * u + w)

    group = 3 if (n_ca - 1) % 3 == 0 else 1

    @pl.loop(0, PIECES)
    def _(hh):
        @pl.when(hh == 0)
        def _():
            paired(5, bd, 0)

        @pl.when(hh == 1)
        def _():
            paired(5, bd, 1)
            reduce_lse(0)

        @pl.loop(0, (n_ca - 1) // group)
        def _(u):
            for w in range(group):
                tile(group * u + w, SQUARE - 1, hh)

        @pl.when(hh == 0)
        def _():
            for v in range((n_ca - 2) * halves, events):
                event(v)
            corner_in(1)

        @pl.when(hh == 1)
        def _():
            share_lse(0)

        for p in range(SQUARE):
            tile(n_ca - 1, p, hh)

    reduce_lse(1)
    logits = logits_ref[...]
    top = jnp.max(jnp.max(logits, axis=0), axis=1, keepdims=True)
    logit_total = top + jnp.log(jnp.sum(jnp.sum(jnp.exp(logits - top[None]), axis=0), axis=1, keepdims=True))

    def finish_lse(hh):
        @pl.loop(1, n)
        def _(k):
            send_lse(k, hh).wait_recv()

        own_lse = lse[hh]
        high = lax.fori_loop(1, n, lambda k, h: jnp.maximum(h, lbuf[k, hh]), own_lse)
        total = lax.fori_loop(1, n, lambda k, x: x + jnp.exp(lbuf[k, hh] - high), jnp.exp(own_lse - high))
        row_total = high + jnp.log(total)
        tot[hh] = row_total
        like_ref[:, hh * part_rows:(hh + 1) * part_rows] = tot[hh, b] - logit_total

        @pl.loop(0, n_ca)
        def _(j):
            peak[j, hh] = jnp.exp(peak[j, hh] - row_total)

    share_lse(1)
    finish_lse(0)

    def info(k):
        j = target(k, a, n_ca)
        way = (j < a).astype(jnp.int32)
        joined = jnp.where(j < a, a < n_ca - 1, a > 0)
        return j, way, joined

    def slot(j, way, owner):
        return jnp.where(jnp.logical_and(j == owner, way == 1), n_ca, j)

    def out_copies(k, h):
        j, way, _ = info(k)
        nbr = jnp.clip(a + 1 - 2 * way, 0, n_ca - 1)
        dev = (nbr, b, m)
        s = slot(j, way, nbr)
        rows = pl.ds(pl.multiple_of(h * rh, rh), rh)
        return (
            remote(sbuf.at[j, rows], rbuf.at[s, rows], msend.at[j, h], mrecv.at[s, h], dev),
            remote(sc.at[j, h], rc.at[s, h], csend.at[j, h], crecv.at[s, h], dev),
        )

    def in_copies(j, way, h):
        nbr = jnp.clip(a - 1 + 2 * way, 0, n_ca - 1)
        dev = (nbr, b, m)
        s = slot(j, way, a)
        rows = pl.ds(pl.multiple_of(h * rh, rh), rh)
        return s, (
            remote(sbuf.at[j, rows], rbuf.at[s, rows], msend.at[j, h], mrecv.at[s, h], dev),
            remote(sc.at[j, h], rc.at[s, h], csend.at[j, h], crecv.at[s, h], dev),
        )

    def start_piece(v):
        for c in out_copies(v // halves, lax.rem(v, halves)):
            c.start()

    def merge(v):
        k, h = v // halves, lax.rem(v, halves)
        j, way, _ = info(k)
        s, copies = in_copies(j, way, h)
        for c in copies:
            c.wait_recv()
        rows = pl.ds(pl.multiple_of(h * rh, rh), rh)
        sbuf[j, rows] = (acc[k, rows] + rbuf[s, rows].astype(F32)).astype(BF16)
        sc[j, h] = crow[k, h] + rc[s, h]

    exports = (n_ca - 1) * halves

    def flush(v):
        @pl.when(jnp.logical_and(jnp.logical_and(v >= 1, v - 1 < exports), jnp.logical_not(info((v - 1) // halves)[2])))
        def _():
            start_piece(jnp.maximum(v - 1, 0))

        w = v - 1 - halves

        @pl.when(jnp.logical_and(w >= 0, info(jnp.maximum(w, 0) // halves)[2]))
        def _():
            start_piece(jnp.maximum(w, 0))

    def weigh(k, h, hh):
        j = target(k, a, n_ca)
        rows = pl.ds(pl.multiple_of(h * rh, rh), rh)
        cols = pl.ds(hh * part_rows, part_rows)
        prod = part = None
        for i in range(SQUARE):
            shares = (ebuf[j, i, rows, cols] * peak[j, hh, i]).astype(BF16)
            wide = shares.astype(F32)
            for q in range(part_rows // 128):
                lane = wide[:, q * 128:(q + 1) * 128]
                part = lane if part is None else part + lane
            p = jnp.dot(shares, feats[i, cols], preferred_element_type=F32)
            prod = p if prod is None else prod + p
        return prod, part

    def settle(v, k, h):
        rows = pl.ds(pl.multiple_of(h * rh, rh), rh)
        crow[k, h] = jnp.sum(cacc[...].T, axis=0, keepdims=True)

        @pl.when(jnp.logical_and(v < exports, jnp.logical_not(info(k)[2])))
        def _():
            j = info(k)[0]
            sbuf[j, rows] = acc[k, rows].astype(BF16)
            sc[j, h] = crow[k, h]

        w = v - halves

        @pl.when(jnp.logical_and(w >= 0, info(jnp.maximum(w, 0) // halves)[2]))
        def _():
            merge(jnp.maximum(w, 0))

    acc[0, :rh], cacc[...] = weigh(0, 0, 0)
    finish_lse(1)
    prod, part = weigh(0, 0, 1)
    acc[0, :rh] += prod
    cacc[...] += part
    settle(0, 0, 0)

    @pl.loop(1, n_ca * halves)
    def _(v):
        k, h = v // halves, lax.rem(v, halves)
        rows = pl.ds(pl.multiple_of(h * rh, rh), rh)
        flush(v)
        prod, part = weigh(k, h, 0)
        acc[k, rows] = prod
        cacc[...] = part
        prod, part = weigh(k, h, 1)
        acc[k, rows] += prod
        cacc[...] += part
        settle(v, k, h)

    first_ref[...] = acc[n_ca - 1, :, d:] + means_ref[...]
    second_ref[...] = acc[n_ca - 1, :, :d] + 1.0 / prec_ref[...] + means_ref[...] * means_ref[...]
    flush(n_ca * halves)

    def join(way, h):
        s, copies = in_copies(a, jnp.int32(way), h)
        for c in copies:
            c.wait_recv()
        rows = pl.ds(h * rh, rh)
        first_ref[rows] += rbuf[s, rows, d:].astype(F32)
        second_ref[rows] += rbuf[s, rows, :d].astype(F32)
        crow[n_ca - 1, h] += rc[s, h]

    for h in range(halves):
        @pl.when(a > 0)
        def _():
            join(0, h)

        @pl.when(a < n_ca - 1)
        def _():
            join(1, h)

    for h in range(halves):
        den_ref[h] = crow[n_ca - 1, h] + 1.0

    @pl.loop(0, exports)
    def _(v):
        for c in out_copies(v // halves, lax.rem(v, halves)):
            c.wait_send()

    for k, i in enumerate((b, b, bd, bx, by, bd)):
        for piece in range(PIECES):
            img_copy(k, i, to_p, piece).wait_send()

    for dist in range(n_ca - 1):
        for way in (0, 1):
            @pl.when(jnp.logical_and(exists(way, dist), has_next(way)))
            def _():
                for h in range(halves):
                    w_copy(way, dist, h, a).wait_send()
                off_copy(way, dist, a).wait_send()

    @pl.loop(1, n)
    def _(k):
        for hh in range(PIECES):
            send_lse(k, hh).wait_send()


def em(images, means, precisions, logits, n_ca, n_mp):
    t, d = images.shape
    r = means.shape[0]
    halves = 2 if r % 32 == 0 else 1
    n = SQUARE * n_mp
    vmem = pl.BlockSpec(memory_space=pltpu.VMEM)
    dma = pltpu.SemaphoreType.DMA
    line = dma((2, n_ca - 1, halves))
    short = dma((2, n_ca - 1))
    return pl.pallas_call(
        functools.partial(em_kernel, n_ca, n_mp, halves),
        out_shape=(
            jax.ShapeDtypeStruct((r, d), F32),
            jax.ShapeDtypeStruct((r, d), F32),
            jax.ShapeDtypeStruct((halves, 1, r // halves), F32),
            jax.ShapeDtypeStruct((1, t), F32),
        ),
        in_specs=[pl.BlockSpec(memory_space=pl.ANY), vmem, vmem, vmem],
        out_specs=(vmem,) * 4,
        scratch_shapes=[
            pltpu.VMEM((SQUARE, t, 2 * d), BF16),
            pltpu.VMEM((n_ca, r, 2 * d), BF16),
            pltpu.VMEM((n_ca, 1, r), F32),
            pltpu.VMEM((n_ca, r, 128), F32),
            pltpu.VMEM((n_ca, SQUARE, r, t), F32),
            pltpu.VMEM((n_ca, PIECES, SQUARE, 1, t // PIECES), F32),
            pltpu.VMEM((n_ca, PIECES, SQUARE, 1, t // PIECES), F32),
            pltpu.VMEM((PIECES, SQUARE, 1, t // PIECES), F32),
            pltpu.VMEM((PIECES, SQUARE, 1, t // PIECES), F32),
            pltpu.VMEM((n, PIECES, SQUARE, 1, t // PIECES), F32),
            pltpu.VMEM((n_ca, r, 2 * d), F32),
            pltpu.VMEM((r // halves, 128), F32),
            pltpu.VMEM((n_ca, halves, 1, r // halves), F32),
            pltpu.VMEM((n_ca, r, 2 * d), BF16),
            pltpu.VMEM((n_ca, halves, 1, r // halves), F32),
            pltpu.VMEM((n_ca + 1, r, 2 * d), BF16),
            pltpu.VMEM((n_ca + 1, halves, 1, r // halves), F32),
            dma((1,)),
            dma((6, PIECES)),
            dma((6, PIECES)),
            line, line, short, short,
            dma((n, PIECES)),
            dma((n, PIECES)),
            dma((n_ca, halves)),
            dma((n_ca + 1, halves)),
            dma((n_ca, halves)),
            dma((n_ca + 1, halves)),
        ],
        compiler_params=pltpu.CompilerParams(
            collective_id=0, has_side_effects=True, vmem_limit_bytes=VMEM_LIMIT
        ),
        name="em",
    )(images, means, precisions, logits.reshape(-1, 1, r))


def finish_kernel(total, first_ref, second_ref, den_ref, like_ref, nm_ref, nv_ref, nw_ref, ll_ref):
    halves, _, rh = den_ref.shape
    for h in range(halves):
        rows = slice(h * rh, (h + 1) * rh)
        den = den_ref[h]
        inv = 1.0 / jnp.broadcast_to(den, (128, rh)).T[:, :1]
        mean = first_ref[rows] * inv
        nm_ref[rows] = mean
        nv_ref[rows] = second_ref[rows] * inv - mean * mean
        nw_ref[h] = jnp.log(den) - jnp.log(jnp.float32(total))
    ll_ref[...] = like_ref[...]


def finish(total, first, second, den, like):
    vmem = pl.BlockSpec(memory_space=pltpu.VMEM)
    return pl.pallas_call(
        functools.partial(finish_kernel, total),
        out_shape=tuple(jax.ShapeDtypeStruct(x.shape, F32) for x in (first, second, den, like)),
        in_specs=[vmem] * 4,
        out_specs=(vmem,) * 4,
        name="finish",
    )(first, second, den, like)


def body(n_ca, n_mp, images, means, precisions, logits):
    t, d = images.shape
    r = means.shape[0]
    total = float(t * n_ca * SQUARE + logits.shape[0])
    outs = em(images, means, precisions, logits, n_ca, n_mp)
    new_means, new_variances, new_log_weights, like = finish(total, *outs)
    return (new_means, new_variances, new_log_weights.reshape(r), like[0])


def solution(mesh):
    n_dp, n_mp = mesh.shape["dp"], mesh.shape["mp"]
    n_ca = n_dp // SQUARE
    split = Mesh(mesh.devices.reshape(n_ca, SQUARE, n_mp), ("ca", "ib", "mp"))
    dp = ("ca", "ib")
    comp = ("mp", "ca", "ib")
    return jax.shard_map(
        functools.partial(body, n_ca, n_mp),
        mesh=split,
        in_specs=(P(dp, None), P(comp, None), P(comp, None), P()),
        out_specs=(P(comp, None), P(comp, None), P(comp), P(dp)),
        check_vma=False,
    )
```

```python
import functools
import math

import jax
import jax.numpy as jnp
from jax import lax
from jax.experimental import pallas as pl
from jax.experimental.pallas import tpu as pltpu
from jax.sharding import Mesh, PartitionSpec as P

MESH = pl.DeviceIdType.MESH
SQUARE = 4
PIECES = 2
TILES = 2
F32 = jnp.float32
BF16 = jnp.bfloat16
VMEM_LIMIT = 65_500_000


def remote(src, dst, send, recv, device):
    return pltpu.make_async_remote_copy(
        src_ref=src, dst_ref=dst, send_sem=send, recv_sem=recv, device_id=device, device_id_type=MESH
    )


def target(k, a, n):
    left, right = a, n - 1 - a
    far, near = jnp.maximum(left, right), jnp.minimum(left, right)
    lead = far - near
    late = jnp.maximum(k - lead, 0)
    dist = jnp.where(k < lead, far - k, near - late // 2)
    to_far = jnp.logical_or(k < lead, lax.rem(late, 2) == 1)
    to_right = jnp.where(right >= left, to_far, jnp.logical_not(to_far))
    return jnp.where(to_right, a + dist, a - dist)


def schedule(n_ca):
    b, c = n_ca - 2, n_ca - 1
    both, near, far = (0, 4), (1, 1), (5, 1)
    shapes = (
        (0, 1, both, 2),
        (1, b, both, 2),
        (0, b, near, 2),
        (b, c, both, 2),
        (b, c, near, 2),
        (0, c, far, 2),
    )
    out, t = [], 0
    for q0, q1, (p0, stride), count in shapes:
        out.append((t, q0, p0, stride, count))
        t += (q1 - q0) * count
    return out, t


def em_kernel(n_ca, n_mp, halves, img_ref, means_hbm, prec_hbm, logits_hbm,
              first_ref, second_ref, den_ref, like_ref,
              means_ref, prec_ref, logits_ref, feats, wall, offall, offcol, ebuf, peak, blk_lse, lse, tot, lbuf, acc, cacc, crow, sbuf, sc, rbuf, rc,
              loc, isend, irecv, wsend, wrecv, osend, orecv, lsend, lrecv, msend, mrecv, csend, crecv):
    a, b, m = lax.axis_index("ca"), lax.axis_index("ib"), lax.axis_index("mp")
    t_rows, d = img_ref.shape
    r = means_hbm.shape[0]
    rh = r // halves
    core = lax.rem(m, 2)
    partner = m + 1 - 2 * core
    bx = b + 1 - 2 * lax.rem(b, 2)
    by = lax.rem(b + 2, 4)
    bd = lax.rem(bx + 2, 4)
    to_x, to_y, to_p = (a, bx, m), (a, by, m), (a, b, partner)
    sub = t_rows // (2 * PIECES)
    part_rows = 2 * sub
    n = SQUARE * n_mp
    me = b * n_mp + m

    def peer(k):
        p = lax.rem(me + k, n)
        return (a, p // n_mp, lax.rem(p, n_mp))

    barrier = pltpu.get_barrier_semaphore()

    @pl.loop(1, n)
    def _(k):
        pl.semaphore_signal(barrier, inc=1, device_id=peer(k), device_id_type=MESH)

    @pl.when(a > 0)
    def _():
        pl.semaphore_signal(barrier, inc=1, device_id=(a - 1, b, m), device_id_type=MESH)

    @pl.when(a < n_ca - 1)
    def _():
        pl.semaphore_signal(barrier, inc=1, device_id=(a + 1, b, m), device_id_type=MESH)

    def image_cols(i, rows):
        return feats.at[i, rows, pl.ds(d, d)]

    own = pltpu.make_async_copy(img_ref, feats.at[b, :, pl.ds(d, d)], loc.at[0])
    fetch = (
        pltpu.make_async_copy(means_hbm, means_ref, loc.at[1]),
        pltpu.make_async_copy(prec_hbm, prec_ref, loc.at[2]),
        pltpu.make_async_copy(logits_hbm, logits_ref, loc.at[3]),
    )
    for c in fetch:
        c.start()
    own.start()
    for c in fetch:
        c.wait()

    means, prec = means_ref[...], prec_ref[...]
    wall[a] = jnp.concatenate([-0.5 * prec.astype(BF16), (means * prec).astype(BF16)], axis=1)
    terms = 0.5 * jnp.sum(jnp.log(prec) - means * means * prec, axis=1, keepdims=True)
    row = jnp.broadcast_to(terms, (r, 128)).T[:1]
    offall[a] = logits_ref[(m * n_ca + a) * SQUARE + b] + row - 0.5 * d * math.log(2.0 * math.pi)

    ends = (a == 0).astype(jnp.int32) + (a == n_ca - 1).astype(jnp.int32)
    pl.semaphore_wait(barrier, n + 1 - ends)

    def img_copy(k, i, dev, piece, first=False):
        rows = pl.ds(pl.multiple_of((piece * 2 + core) * sub, sub), sub)
        dst = image_cols(i, rows)
        return remote(img_ref.at[rows] if first else dst, dst, isend.at[k, piece], irecv.at[k, piece], dev)

    def has_next(way):
        return a < n_ca - 1 if way == 0 else a > 0

    def hop(way, dist, sender):
        blk = jnp.clip(sender - dist + 2 * way * dist, 0, n_ca - 1)
        return blk, (jnp.clip(a + 1 - 2 * way, 0, n_ca - 1), b, m)

    def w_copy(way, dist, h, sender):
        blk, dev = hop(way, dist, sender)
        block = wall.at[blk, pl.ds(h * rh, rh)]
        return remote(block, block, wsend.at[way, dist, h], wrecv.at[way, dist, h], dev)

    def off_copy(way, dist, sender):
        blk, dev = hop(way, dist, sender)
        return remote(offall.at[blk], offall.at[blk], osend.at[way, dist], orecv.at[way, dist], dev)

    def exists(way, dist):
        blk = a - dist + 2 * way * dist
        return jnp.logical_and(blk >= 0, blk < n_ca)

    def forward(way, dist, h):
        @pl.when(has_next(way))
        def _():
            w_copy(way, dist, h, a).start()
            if h == 0:
                off_copy(way, dist, a).start()

    for piece in range(PIECES):
        img_copy(0, b, to_x, piece, True).start()
        img_copy(1, b, to_y, piece, True).start()
    for h in range(halves):
        for way in (0, 1):
            forward(way, 0, h)

    def column(blk):
        offcol[blk] = jnp.broadcast_to(offall[blk], (128, r)).T

    def event(u):
        dist, h = u // halves + 1, u % halves
        for way in (0, 1):
            @pl.when(exists(way, dist))
            def _():
                sender = a - 1 + 2 * way
                w_copy(way, dist - 1, h, sender).wait_recv()
                if h == 0:
                    off_copy(way, dist - 1, sender).wait_recv()
                if dist < n_ca - 1:
                    forward(way, dist, h)
                if h == 0:
                    column(hop(way, dist - 1, sender)[0])

    def images_in(piece):
        img_copy(0, bx, to_x, piece).wait_recv()
        img_copy(3, bx, to_p, piece).start()

        @pl.when(core == 0)
        def _():
            img_copy(2, bx, to_y, piece).start()

        img_copy(1, by, to_y, piece).wait_recv()
        img_copy(4, by, to_p, piece).start()

        @pl.when(core == 1)
        def _():
            img_copy(2, by, to_x, piece).start()

    def corner_in(piece):
        img_copy(2, bd, to_x, piece).wait_recv()
        img_copy(5, bd, to_p, piece).start()

    def square(i, piece):
        rows = pl.ds(pl.multiple_of(piece * part_rows, part_rows), part_rows)
        wide = feats[i, rows, d:].astype(F32)
        feats[i, rows, :d] = (wide * wide).astype(BF16)

    def paired(k, i, piece):
        img_copy(k, i, to_p, piece).wait_recv()
        square(i, piece)

    own.wait()
    column(a)
    for piece in range(PIECES):
        square(b, piece)

    def shard(p):
        return jnp.where(p == 0, b, jnp.where(p == 1, bx, jnp.where(p == 2, by, bd)))

    def send_lse(k, hh):
        return remote(lse.at[hh], lbuf.at[k, hh], lsend.at[k, hh], lrecv.at[k, hh], peer(k))

    def log_sum(rows):
        high = functools.reduce(jnp.maximum, rows)
        return high + jnp.log(functools.reduce(jnp.add, [jnp.exp(x - high) for x in rows]))

    def reduce_lse(hh):
        lse[hh] = log_sum([blk_lse[k, hh] for k in range(n_ca)])

    def share_lse(hh):
        @pl.loop(1, n)
        def _(k):
            send_lse(k, hh).start()

    rects, tiles = schedule(n_ca)
    pair = [x[0] // TILES for x in rects]
    events = (n_ca - 1) * halves

    def tile(q, p, hh):
        j = target(n_ca - 1 - q, a, n_ca)
        i = shard(p)
        cols = pl.ds(pl.multiple_of(hh * part_rows, part_rows), part_rows)
        s = lax.dot_general(wall[j], feats[i, cols], (((1,), (1,)), ((), ())), preferred_element_type=F32)
        s = s + offcol[j][:, :1]
        top = jnp.max(s, axis=0, keepdims=True)
        e = jnp.exp(s - top)
        ebuf[j, i, :, cols] = e
        peak[j, hh, i] = top
        blk_lse[j, hh, i] = top + jnp.log(jnp.sum(e, axis=0, keepdims=True))

    def early_tile(t):
        q, part = t, t
        for t0, q0, p0, stride, count in rects:
            here = t >= t0
            s = jnp.maximum(t - t0, 0)
            q = jnp.where(here, q0 + s // count, q)
            part = jnp.where(here, p0 + stride * lax.rem(s, count), part)
        hh = part // SQUARE
        tile(q, part - SQUARE * hh, hh)

    @pl.loop(0, tiles // TILES)
    def _(u):
        @pl.when(u == pair[1])
        def _():
            for v in range((n_ca - 3) * halves):
                event(v)
            images_in(0)

        @pl.when(u == pair[2])
        def _():
            paired(3, bx, 0)
            paired(4, by, 0)

        @pl.when(u == pair[3])
        def _():
            for v in range((n_ca - 3) * halves, (n_ca - 2) * halves):
                event(v)
            images_in(1)

        @pl.when(u == pair[5])
        def _():
            paired(3, bx, 1)
            paired(4, by, 1)

        @pl.when(u == tiles // TILES - 1)
        def _():
            corner_in(0)

        for w in range(TILES):
            early_tile(TILES * u + w)

    group = 3 if (n_ca - 1) % 3 == 0 else 1

    @pl.loop(0, PIECES)
    def _(hh):
        @pl.when(hh == 0)
        def _():
            paired(5, bd, 0)

        @pl.when(hh == 1)
        def _():
            paired(5, bd, 1)
            reduce_lse(0)

        @pl.loop(0, (n_ca - 1) // group)
        def _(u):
            for w in range(group):
                tile(group * u + w, SQUARE - 1, hh)

        @pl.when(hh == 0)
        def _():
            for v in range((n_ca - 2) * halves, events):
                event(v)
            corner_in(1)

        @pl.when(hh == 1)
        def _():
            share_lse(0)

        for p in range(SQUARE):
            tile(n_ca - 1, p, hh)

    def finish_lse(hh):
        @pl.loop(1, n)
        def _(k):
            send_lse(k, hh).wait_recv()

        tot[hh] = log_sum([lse[hh]] + [lbuf[k, hh] for k in range(1, n)])

    reduce_lse(1)
    finish_lse(0)
    share_lse(1)

    def info(k):
        j = target(k, a, n_ca)
        way = (j < a).astype(jnp.int32)
        joined = jnp.where(j < a, a < n_ca - 1, a > 0)
        return j, way, joined

    def slot(j, way, owner):
        return jnp.where(jnp.logical_and(j == owner, way == 1), n_ca, j)

    def out_copies(k, h):
        j, way, _ = info(k)
        nbr = jnp.clip(a + 1 - 2 * way, 0, n_ca - 1)
        dev = (nbr, b, m)
        s = slot(j, way, nbr)
        rows = pl.ds(pl.multiple_of(h * rh, rh), rh)
        return (
            remote(sbuf.at[j, rows], rbuf.at[s, rows], msend.at[j, h], mrecv.at[s, h], dev),
            remote(sc.at[j, h], rc.at[s, h], csend.at[j, h], crecv.at[s, h], dev),
        )

    def in_copies(j, way, h):
        nbr = jnp.clip(a - 1 + 2 * way, 0, n_ca - 1)
        dev = (nbr, b, m)
        s = slot(j, way, a)
        rows = pl.ds(pl.multiple_of(h * rh, rh), rh)
        return s, (
            remote(sbuf.at[j, rows], rbuf.at[s, rows], msend.at[j, h], mrecv.at[s, h], dev),
            remote(sc.at[j, h], rc.at[s, h], csend.at[j, h], crecv.at[s, h], dev),
        )

    def start_piece(v):
        for c in out_copies(v // halves, lax.rem(v, halves)):
            c.start()

    def merge(v):
        k, h = v // halves, lax.rem(v, halves)
        j, way, _ = info(k)
        s, copies = in_copies(j, way, h)
        for c in copies:
            c.wait_recv()
        rows = pl.ds(pl.multiple_of(h * rh, rh), rh)
        sbuf[j, rows] = (acc[k, rows] + rbuf[s, rows].astype(F32)).astype(BF16)
        sc[j, h] = crow[k, h] + rc[s, h]

    exports = (n_ca - 1) * halves

    def flush(v):
        @pl.when(jnp.logical_and(jnp.logical_and(v >= 1, v - 1 < exports), jnp.logical_not(info((v - 1) // halves)[2])))
        def _():
            start_piece(jnp.maximum(v - 1, 0))

        w = v - 1 - halves

        @pl.when(jnp.logical_and(w >= 0, info(jnp.maximum(w, 0) // halves)[2]))
        def _():
            start_piece(jnp.maximum(w, 0))

    def weigh(k, h, hh):
        j = target(k, a, n_ca)
        rows = pl.ds(pl.multiple_of(h * rh, rh), rh)
        cols = pl.ds(hh * part_rows, part_rows)
        prod = part = None
        for i in range(SQUARE):
            factor = jnp.exp(peak[j, hh, i] - tot[hh, i])
            shares = (ebuf[j, i, rows, cols] * factor).astype(BF16)
            wide = shares.astype(F32)
            for q in range(part_rows // 128):
                lane = wide[:, q * 128:(q + 1) * 128]
                part = lane if part is None else part + lane
            p = jnp.dot(shares, feats[i, cols], preferred_element_type=F32)
            prod = p if prod is None else prod + p
        return prod, part

    def settle(v, k, h):
        rows = pl.ds(pl.multiple_of(h * rh, rh), rh)
        crow[k, h] = jnp.sum(cacc[...].T, axis=0, keepdims=True)

        @pl.when(jnp.logical_and(v < exports, jnp.logical_not(info(k)[2])))
        def _():
            j = info(k)[0]
            sbuf[j, rows] = acc[k, rows].astype(BF16)
            sc[j, h] = crow[k, h]

        w = v - halves

        @pl.when(jnp.logical_and(w >= 0, info(jnp.maximum(w, 0) // halves)[2]))
        def _():
            merge(jnp.maximum(w, 0))

    acc[0, :rh], cacc[...] = weigh(0, 0, 0)
    finish_lse(1)
    prod, part = weigh(0, 0, 1)
    acc[0, :rh] += prod
    cacc[...] += part
    settle(0, 0, 0)

    @pl.loop(1, n_ca * halves)
    def _(v):
        k, h = v // halves, lax.rem(v, halves)
        rows = pl.ds(pl.multiple_of(h * rh, rh), rh)
        flush(v)
        prod, part = weigh(k, h, 0)
        acc[k, rows] = prod
        cacc[...] = part
        prod, part = weigh(k, h, 1)
        acc[k, rows] += prod
        cacc[...] += part
        settle(v, k, h)

    first_ref[...] = acc[n_ca - 1, :, d:] + means_ref[...]
    second_ref[...] = acc[n_ca - 1, :, :d] + 1.0 / prec_ref[...] + means_ref[...] * means_ref[...]
    flush(n_ca * halves)

    logits = logits_ref[...]
    top = jnp.max(jnp.max(logits, axis=0), axis=1, keepdims=True)
    logit_total = top + jnp.log(jnp.sum(jnp.sum(jnp.exp(logits - top[None]), axis=0), axis=1, keepdims=True))
    for hh in range(PIECES):
        like_ref[:, hh * part_rows:(hh + 1) * part_rows] = tot[hh, b] - logit_total

    def join(way, h):
        s, copies = in_copies(a, jnp.int32(way), h)
        for c in copies:
            c.wait_recv()
        rows = pl.ds(h * rh, rh)
        first_ref[rows] += rbuf[s, rows, d:].astype(F32)
        second_ref[rows] += rbuf[s, rows, :d].astype(F32)
        crow[n_ca - 1, h] += rc[s, h]

    for h in range(halves):
        @pl.when(a > 0)
        def _():
            join(0, h)

        @pl.when(a < n_ca - 1)
        def _():
            join(1, h)

    for h in range(halves):
        den_ref[h] = crow[n_ca - 1, h] + 1.0

    @pl.loop(0, exports)
    def _(v):
        for c in out_copies(v // halves, lax.rem(v, halves)):
            c.wait_send()

    for k, i in enumerate((b, b, bd, bx, by, bd)):
        for piece in range(PIECES):
            img_copy(k, i, to_p, piece).wait_send()

    for dist in range(n_ca - 1):
        for way in (0, 1):
            @pl.when(jnp.logical_and(exists(way, dist), has_next(way)))
            def _():
                for h in range(halves):
                    w_copy(way, dist, h, a).wait_send()
                off_copy(way, dist, a).wait_send()

    @pl.loop(1, n)
    def _(k):
        for hh in range(PIECES):
            send_lse(k, hh).wait_send()


def em(images, means, precisions, logits, n_ca, n_mp):
    t, d = images.shape
    r = means.shape[0]
    halves = 2 if r % 32 == 0 else 1
    n = SQUARE * n_mp
    vmem = pl.BlockSpec(memory_space=pltpu.VMEM)
    dma = pltpu.SemaphoreType.DMA
    line = dma((2, n_ca - 1, halves))
    short = dma((2, n_ca - 1))
    return pl.pallas_call(
        functools.partial(em_kernel, n_ca, n_mp, halves),
        out_shape=(
            pltpu.VMEM((r, d), F32),
            pltpu.VMEM((r, d), F32),
            pltpu.VMEM((halves, 1, r // halves), F32),
            pltpu.VMEM((1, t), F32),
        ),
        in_specs=[pl.BlockSpec(memory_space=pl.ANY)] * 4,
        out_specs=(vmem,) * 4,
        scratch_shapes=[
            pltpu.VMEM((r, d), F32),
            pltpu.VMEM((r, d), F32),
            pltpu.VMEM((logits.shape[0] // r, 1, r), F32),
            pltpu.VMEM((SQUARE, t, 2 * d), BF16),
            pltpu.VMEM((n_ca, r, 2 * d), BF16),
            pltpu.VMEM((n_ca, 1, r), F32),
            pltpu.VMEM((n_ca, r, 128), F32),
            pltpu.VMEM((n_ca, SQUARE, r, t), F32),
            pltpu.VMEM((n_ca, PIECES, SQUARE, 1, t // PIECES), F32),
            pltpu.VMEM((n_ca, PIECES, SQUARE, 1, t // PIECES), F32),
            pltpu.VMEM((PIECES, SQUARE, 1, t // PIECES), F32),
            pltpu.VMEM((PIECES, SQUARE, 1, t // PIECES), F32),
            pltpu.VMEM((n, PIECES, SQUARE, 1, t // PIECES), F32),
            pltpu.VMEM((n_ca, r, 2 * d), F32),
            pltpu.VMEM((r // halves, 128), F32),
            pltpu.VMEM((n_ca, halves, 1, r // halves), F32),
            pltpu.VMEM((n_ca, r, 2 * d), BF16),
            pltpu.VMEM((n_ca, halves, 1, r // halves), F32),
            pltpu.VMEM((n_ca + 1, r, 2 * d), BF16),
            pltpu.VMEM((n_ca + 1, halves, 1, r // halves), F32),
            dma((4,)),
            dma((6, PIECES)),
            dma((6, PIECES)),
            line, line, short, short,
            dma((n, PIECES)),
            dma((n, PIECES)),
            dma((n_ca, halves)),
            dma((n_ca + 1, halves)),
            dma((n_ca, halves)),
            dma((n_ca + 1, halves)),
        ],
        compiler_params=pltpu.CompilerParams(
            collective_id=0, has_side_effects=True, vmem_limit_bytes=VMEM_LIMIT
        ),
        name="em",
    )(images, means, precisions, logits.reshape(-1, 1, r))


def finish_kernel(total, first_ref, second_ref, den_ref, like_ref, nm_ref, nv_ref, nw_ref, ll_ref):
    halves, _, rh = den_ref.shape
    for h in range(halves):
        rows = slice(h * rh, (h + 1) * rh)
        den = den_ref[h]
        inv = 1.0 / jnp.broadcast_to(den, (128, rh)).T[:, :1]
        mean = first_ref[rows] * inv
        nm_ref[rows] = mean
        nv_ref[rows] = second_ref[rows] * inv - mean * mean
        nw_ref[h] = jnp.log(den) - jnp.log(jnp.float32(total))
    ll_ref[...] = like_ref[...]


def finish(total, first, second, den, like):
    vmem = pl.BlockSpec(memory_space=pltpu.VMEM)
    return pl.pallas_call(
        functools.partial(finish_kernel, total),
        out_shape=tuple(jax.ShapeDtypeStruct(x.shape, F32) for x in (first, second, den, like)),
        in_specs=[vmem] * 4,
        out_specs=(vmem,) * 4,
        name="finish",
    )(*(pltpu.with_memory_space_constraint(x, pltpu.VMEM) for x in (first, second, den, like)))


def body(n_ca, n_mp, images, means, precisions, logits):
    t, d = images.shape
    r = means.shape[0]
    total = float(t * n_ca * SQUARE + logits.shape[0])
    outs = em(images, means, precisions, logits, n_ca, n_mp)
    new_means, new_variances, new_log_weights, like = finish(total, *outs)
    return (new_means, new_variances, new_log_weights.reshape(r), like[0])


def solution(mesh):
    n_dp, n_mp = mesh.shape["dp"], mesh.shape["mp"]
    n_ca = n_dp // SQUARE
    split = Mesh(mesh.devices.reshape(n_ca, SQUARE, n_mp), ("ca", "ib", "mp"))
    dp = ("ca", "ib")
    comp = ("mp", "ca", "ib")
    return jax.shard_map(
        functools.partial(body, n_ca, n_mp),
        mesh=split,
        in_specs=(P(dp, None), P(comp, None), P(comp, None), P()),
        out_specs=(P(comp, None), P(comp, None), P(comp), P(dp)),
        check_vma=False,
    )
```

```python
import functools
import math

import jax
import jax.numpy as jnp
from jax import lax
from jax.experimental import pallas as pl
from jax.experimental.pallas import tpu as pltpu
from jax.sharding import Mesh, PartitionSpec as P

MESH = pl.DeviceIdType.MESH
SQUARE = 4
PIECES = 2
TILES = 2
F32 = jnp.float32
BF16 = jnp.bfloat16
VMEM_LIMIT = 65_500_000


def remote(src, dst, send, recv, device):
    return pltpu.make_async_remote_copy(
        src_ref=src, dst_ref=dst, send_sem=send, recv_sem=recv, device_id=device, device_id_type=MESH
    )


def target(k, a, n):
    left, right = a, n - 1 - a
    far, near = jnp.maximum(left, right), jnp.minimum(left, right)
    lead = far - near
    late = jnp.maximum(k - lead, 0)
    dist = jnp.where(k < lead, far - k, near - late // 2)
    to_far = jnp.logical_or(k < lead, lax.rem(late, 2) == 1)
    to_right = jnp.where(right >= left, to_far, jnp.logical_not(to_far))
    return jnp.where(to_right, a + dist, a - dist)


def schedule(n_ca):
    b, c = n_ca - 2, n_ca - 1
    both, near, far = (0, 4), (1, 1), (5, 1)
    shapes = (
        (0, 1, both, 2),
        (1, b, both, 2),
        (0, b, near, 2),
        (b, c, both, 2),
        (b, c, near, 2),
        (0, c, far, 2),
    )
    out, t = [], 0
    for q0, q1, (p0, stride), count in shapes:
        out.append((t, q0, p0, stride, count))
        t += (q1 - q0) * count
    return out, t


def em_kernel(n_ca, n_mp, halves, img_ref, means_hbm, prec_hbm, logits_hbm,
              first_ref, second_ref, den_ref, like_ref,
              means_ref, prec_ref, logits_ref, feats, wall, offall, offcol, ebuf, peak, blk_lse, lse, tot, lbuf, acc, cacc, crow, sbuf, sc, rbuf, rc,
              loc, isend, irecv, wsend, wrecv, osend, orecv, lsend, lrecv, msend, mrecv, csend, crecv):
    a, b, m = lax.axis_index("ca"), lax.axis_index("ib"), lax.axis_index("mp")
    t_rows, d = img_ref.shape
    r = means_hbm.shape[0]
    rh = r // halves
    core = lax.rem(m, 2)
    partner = m + 1 - 2 * core
    bx = b + 1 - 2 * lax.rem(b, 2)
    by = lax.rem(b + 2, 4)
    bd = lax.rem(bx + 2, 4)
    to_x, to_y, to_p = (a, bx, m), (a, by, m), (a, b, partner)
    sub = t_rows // (2 * PIECES)
    part_rows = 2 * sub
    n = SQUARE * n_mp
    me = b * n_mp + m

    def peer(k):
        p = lax.rem(me + k, n)
        return (a, p // n_mp, lax.rem(p, n_mp))

    barrier = pltpu.get_barrier_semaphore()

    @pl.loop(1, n)
    def _(k):
        pl.semaphore_signal(barrier, inc=1, device_id=peer(k), device_id_type=MESH)

    @pl.when(a > 0)
    def _():
        pl.semaphore_signal(barrier, inc=1, device_id=(a - 1, b, m), device_id_type=MESH)

    @pl.when(a < n_ca - 1)
    def _():
        pl.semaphore_signal(barrier, inc=1, device_id=(a + 1, b, m), device_id_type=MESH)

    def image_cols(i, rows):
        return feats.at[i, rows, pl.ds(d, d)]

    own = pltpu.make_async_copy(img_ref, feats.at[b, :, pl.ds(d, d)], loc.at[0])
    fetch = (
        pltpu.make_async_copy(means_hbm, means_ref, loc.at[1]),
        pltpu.make_async_copy(prec_hbm, prec_ref, loc.at[2]),
        pltpu.make_async_copy(logits_hbm, logits_ref, loc.at[3]),
    )
    for c in fetch:
        c.start()
    own.start()
    for c in fetch:
        c.wait()

    means, prec = means_ref[...], prec_ref[...]
    wall[a] = jnp.concatenate([-0.5 * prec.astype(BF16), (means * prec).astype(BF16)], axis=1)
    terms = 0.5 * jnp.sum(jnp.log(prec) - means * means * prec, axis=1, keepdims=True)
    row = jnp.broadcast_to(terms, (r, 128)).T[:1]
    offall[a] = logits_ref[(m * n_ca + a) * SQUARE + b] + row - 0.5 * d * math.log(2.0 * math.pi)

    ends = (a == 0).astype(jnp.int32) + (a == n_ca - 1).astype(jnp.int32)
    pl.semaphore_wait(barrier, n + 1 - ends)

    def img_copy(k, i, dev, piece, first=False):
        rows = pl.ds(pl.multiple_of((piece * 2 + core) * sub, sub), sub)
        dst = image_cols(i, rows)
        return remote(img_ref.at[rows] if first else dst, dst, isend.at[k, piece], irecv.at[k, piece], dev)

    def has_next(way):
        return a < n_ca - 1 if way == 0 else a > 0

    def hop(way, dist, sender):
        blk = jnp.clip(sender - dist + 2 * way * dist, 0, n_ca - 1)
        return blk, (jnp.clip(a + 1 - 2 * way, 0, n_ca - 1), b, m)

    def w_copy(way, dist, h, sender):
        blk, dev = hop(way, dist, sender)
        block = wall.at[blk, pl.ds(h * rh, rh)]
        return remote(block, block, wsend.at[way, dist, h], wrecv.at[way, dist, h], dev)

    def off_copy(way, dist, sender):
        blk, dev = hop(way, dist, sender)
        return remote(offall.at[blk], offall.at[blk], osend.at[way, dist], orecv.at[way, dist], dev)

    def exists(way, dist):
        blk = a - dist + 2 * way * dist
        return jnp.logical_and(blk >= 0, blk < n_ca)

    def forward(way, dist, h):
        @pl.when(has_next(way))
        def _():
            w_copy(way, dist, h, a).start()
            if h == 0:
                off_copy(way, dist, a).start()

    for piece in range(PIECES):
        img_copy(0, b, to_x, piece, True).start()
        img_copy(1, b, to_y, piece, True).start()
    for h in range(halves):
        for way in (0, 1):
            forward(way, 0, h)

    def column(blk):
        offcol[blk] = jnp.broadcast_to(offall[blk], (128, r)).T

    def event(u):
        dist, h = u // halves + 1, u % halves
        for way in (0, 1):
            @pl.when(exists(way, dist))
            def _():
                sender = a - 1 + 2 * way
                w_copy(way, dist - 1, h, sender).wait_recv()
                if h == 0:
                    off_copy(way, dist - 1, sender).wait_recv()
                if dist < n_ca - 1:
                    forward(way, dist, h)
                if h == 0:
                    column(hop(way, dist - 1, sender)[0])

    def images_in(piece):
        img_copy(0, bx, to_x, piece).wait_recv()
        img_copy(3, bx, to_p, piece).start()

        @pl.when(core == 0)
        def _():
            img_copy(2, bx, to_y, piece).start()

        img_copy(1, by, to_y, piece).wait_recv()
        img_copy(4, by, to_p, piece).start()

        @pl.when(core == 1)
        def _():
            img_copy(2, by, to_x, piece).start()

    def corner_in(piece):
        img_copy(2, bd, to_x, piece).wait_recv()
        img_copy(5, bd, to_p, piece).start()

    def square(i, piece):
        rows = pl.ds(pl.multiple_of(piece * part_rows, part_rows), part_rows)
        wide = feats[i, rows, d:].astype(F32)
        feats[i, rows, :d] = (wide * wide).astype(BF16)

    def paired(k, i, piece):
        img_copy(k, i, to_p, piece).wait_recv()
        square(i, piece)

    own.wait()
    column(a)
    for piece in range(PIECES):
        square(b, piece)

    def shard(p):
        return jnp.where(p == 0, b, jnp.where(p == 1, bx, jnp.where(p == 2, by, bd)))

    def send_lse(k, hh):
        return remote(lse.at[hh], lbuf.at[k, hh], lsend.at[k, hh], lrecv.at[k, hh], peer(k))

    def log_sum(rows):
        high = functools.reduce(jnp.maximum, rows)
        return high + jnp.log(functools.reduce(jnp.add, [jnp.exp(x - high) for x in rows]))

    def reduce_lse(hh):
        lse[hh] = log_sum([blk_lse[k, hh] for k in range(n_ca)])

    def share_lse(hh):
        @pl.loop(1, n)
        def _(k):
            send_lse(k, hh).start()

    rects, tiles = schedule(n_ca)
    pair = [x[0] // TILES for x in rects]
    events = (n_ca - 1) * halves

    def tile(q, p, hh):
        j = target(n_ca - 1 - q, a, n_ca)
        i = shard(p)
        cols = pl.ds(pl.multiple_of(hh * part_rows, part_rows), part_rows)
        s = lax.dot_general(wall[j], feats[i, cols], (((1,), (1,)), ((), ())), preferred_element_type=F32)
        s = s + offcol[j][:, :1]
        top = jnp.max(s, axis=0, keepdims=True)
        e = jnp.exp(s - top)
        ebuf[j, i, :, cols] = e
        peak[j, hh, i] = top
        blk_lse[j, hh, i] = top + jnp.log(jnp.sum(e, axis=0, keepdims=True))

    def early_tile(t):
        q, part = t, t
        for t0, q0, p0, stride, count in rects:
            here = t >= t0
            s = jnp.maximum(t - t0, 0)
            q = jnp.where(here, q0 + s // count, q)
            part = jnp.where(here, p0 + stride * lax.rem(s, count), part)
        hh = part // SQUARE
        tile(q, part - SQUARE * hh, hh)

    @pl.loop(0, tiles // TILES)
    def _(u):
        @pl.when(u == pair[1])
        def _():
            for v in range((n_ca - 3) * halves):
                event(v)
            images_in(0)

        @pl.when(u == pair[2])
        def _():
            paired(3, bx, 0)
            paired(4, by, 0)

        @pl.when(u == pair[3])
        def _():
            for v in range((n_ca - 3) * halves, (n_ca - 2) * halves):
                event(v)
            images_in(1)

        @pl.when(u == pair[5])
        def _():
            paired(3, bx, 1)
            paired(4, by, 1)

        @pl.when(u == tiles // TILES - 1)
        def _():
            corner_in(0)

        for w in range(TILES):
            early_tile(TILES * u + w)

    group = 3 if (n_ca - 1) % 3 == 0 else 1
    square_tail = n_ca == SQUARE

    @pl.loop(0, PIECES)
    def _(hh):
        @pl.when(hh == 0)
        def _():
            paired(5, bd, 0)

        @pl.when(hh == 1)
        def _():
            if not square_tail:
                paired(5, bd, 1)
            reduce_lse(0)

        def tail(q, p):
            if square_tail:
                first = hh == 0
                q, p = jnp.where(first, q, p), jnp.where(first, p, q)
            tile(q, p, hh)

        @pl.loop(0, (n_ca - 1) // group)
        def _(u):
            for w in range(group):
                tail(group * u + w, SQUARE - 1)

        @pl.when(hh == 0)
        def _():
            for v in range((n_ca - 2) * halves, events):
                event(v)
            corner_in(1)

        @pl.when(hh == 1)
        def _():
            share_lse(0)
            if square_tail:
                paired(5, bd, 1)

        for p in range(SQUARE):
            tail(n_ca - 1, p)

    def finish_lse(hh):
        @pl.loop(1, n)
        def _(k):
            send_lse(k, hh).wait_recv()

        tot[hh] = log_sum([lse[hh]] + [lbuf[k, hh] for k in range(1, n)])

    def sent_lse(hh):
        @pl.loop(1, n)
        def _(k):
            send_lse(k, hh).wait_send()

    reduce_lse(1)
    sent_lse(0)
    share_lse(1)
    finish_lse(0)

    def info(k):
        j = target(k, a, n_ca)
        way = (j < a).astype(jnp.int32)
        joined = jnp.where(j < a, a < n_ca - 1, a > 0)
        return j, way, joined

    def slot(j, way, owner):
        return jnp.where(jnp.logical_and(j == owner, way == 1), n_ca, j)

    def out_copies(k, h):
        j, way, _ = info(k)
        nbr = jnp.clip(a + 1 - 2 * way, 0, n_ca - 1)
        dev = (nbr, b, m)
        s = slot(j, way, nbr)
        rows = pl.ds(pl.multiple_of(h * rh, rh), rh)
        return (
            remote(sbuf.at[j, rows], rbuf.at[s, rows], msend.at[j, h], mrecv.at[s, h], dev),
            remote(sc.at[j, h], rc.at[s, h], csend.at[j, h], crecv.at[s, h], dev),
        )

    def in_copies(j, way, h):
        nbr = jnp.clip(a - 1 + 2 * way, 0, n_ca - 1)
        dev = (nbr, b, m)
        s = slot(j, way, a)
        rows = pl.ds(pl.multiple_of(h * rh, rh), rh)
        return s, (
            remote(sbuf.at[j, rows], rbuf.at[s, rows], msend.at[j, h], mrecv.at[s, h], dev),
            remote(sc.at[j, h], rc.at[s, h], csend.at[j, h], crecv.at[s, h], dev),
        )

    def start_piece(v):
        for c in out_copies(v // halves, lax.rem(v, halves)):
            c.start()

    def merge(v):
        k, h = v // halves, lax.rem(v, halves)
        j, way, _ = info(k)
        s, copies = in_copies(j, way, h)
        for c in copies:
            c.wait_recv()
        rows = pl.ds(pl.multiple_of(h * rh, rh), rh)
        sbuf[j, rows] = (acc[k, rows] + rbuf[s, rows].astype(F32)).astype(BF16)
        sc[j, h] = crow[k, h] + rc[s, h]

    exports = (n_ca - 1) * halves

    def flush(v):
        @pl.when(jnp.logical_and(jnp.logical_and(v >= 1, v - 1 < exports), jnp.logical_not(info((v - 1) // halves)[2])))
        def _():
            start_piece(jnp.maximum(v - 1, 0))

        w = v - 1 - halves

        @pl.when(jnp.logical_and(w >= 0, info(jnp.maximum(w, 0) // halves)[2]))
        def _():
            start_piece(jnp.maximum(w, 0))

    def weigh(k, h, hh):
        j = target(k, a, n_ca)
        rows = pl.ds(pl.multiple_of(h * rh, rh), rh)
        cols = pl.ds(hh * part_rows, part_rows)
        prod = part = None
        for i in range(SQUARE):
            factor = jnp.exp(peak[j, hh, i] - tot[hh, i])
            shares = (ebuf[j, i, rows, cols] * factor).astype(BF16)
            wide = shares.astype(F32)
            for q in range(part_rows // 128):
                lane = wide[:, q * 128:(q + 1) * 128]
                part = lane if part is None else part + lane
            p = jnp.dot(shares, feats[i, cols], preferred_element_type=F32)
            prod = p if prod is None else prod + p
        return prod, part

    def settle(v, k, h):
        rows = pl.ds(pl.multiple_of(h * rh, rh), rh)
        crow[k, h] = jnp.sum(cacc[...].T, axis=0, keepdims=True)

        @pl.when(jnp.logical_and(v < exports, jnp.logical_not(info(k)[2])))
        def _():
            j = info(k)[0]
            sbuf[j, rows] = acc[k, rows].astype(BF16)
            sc[j, h] = crow[k, h]

        w = v - halves

        @pl.when(jnp.logical_and(w >= 0, info(jnp.maximum(w, 0) // halves)[2]))
        def _():
            merge(jnp.maximum(w, 0))

    acc[0, :rh], cacc[...] = weigh(0, 0, 0)
    finish_lse(1)
    prod, part = weigh(0, 0, 1)
    acc[0, :rh] += prod
    cacc[...] += part
    settle(0, 0, 0)

    @pl.loop(1, n_ca * halves)
    def _(v):
        k, h = v // halves, lax.rem(v, halves)
        rows = pl.ds(pl.multiple_of(h * rh, rh), rh)
        flush(v)
        prod, part = weigh(k, h, 0)
        acc[k, rows] = prod
        cacc[...] = part
        prod, part = weigh(k, h, 1)
        acc[k, rows] += prod
        cacc[...] += part
        settle(v, k, h)

    first_ref[...] = acc[n_ca - 1, :, d:] + means_ref[...]
    second_ref[...] = acc[n_ca - 1, :, :d] + 1.0 / prec_ref[...] + means_ref[...] * means_ref[...]
    flush(n_ca * halves)

    logits = logits_ref[...]
    top = jnp.max(jnp.max(logits, axis=0), axis=1, keepdims=True)
    logit_total = top + jnp.log(jnp.sum(jnp.sum(jnp.exp(logits - top[None]), axis=0), axis=1, keepdims=True))
    for hh in range(PIECES):
        like_ref[:, hh * part_rows:(hh + 1) * part_rows] = tot[hh, b] - logit_total

    def join(way, h):
        s, copies = in_copies(a, jnp.int32(way), h)
        for c in copies:
            c.wait_recv()
        rows = pl.ds(h * rh, rh)
        first_ref[rows] += rbuf[s, rows, d:].astype(F32)
        second_ref[rows] += rbuf[s, rows, :d].astype(F32)
        crow[n_ca - 1, h] += rc[s, h]

    for h in range(halves):
        @pl.when(a > 0)
        def _():
            join(0, h)

        @pl.when(a < n_ca - 1)
        def _():
            join(1, h)

    for h in range(halves):
        den_ref[h] = crow[n_ca - 1, h] + 1.0

    @pl.loop(0, exports)
    def _(v):
        for c in out_copies(v // halves, lax.rem(v, halves)):
            c.wait_send()

    for k, i in enumerate((b, b, bd, bx, by, bd)):
        for piece in range(PIECES):
            img_copy(k, i, to_p, piece).wait_send()

    for dist in range(n_ca - 1):
        for way in (0, 1):
            @pl.when(jnp.logical_and(exists(way, dist), has_next(way)))
            def _():
                for h in range(halves):
                    w_copy(way, dist, h, a).wait_send()
                off_copy(way, dist, a).wait_send()

    sent_lse(1)


def em(images, means, precisions, logits, n_ca, n_mp):
    t, d = images.shape
    r = means.shape[0]
    halves = 2 if r % 32 == 0 else 1
    n = SQUARE * n_mp
    vmem = pl.BlockSpec(memory_space=pltpu.VMEM)
    dma = pltpu.SemaphoreType.DMA
    line = dma((2, n_ca - 1, halves))
    short = dma((2, n_ca - 1))
    return pl.pallas_call(
        functools.partial(em_kernel, n_ca, n_mp, halves),
        out_shape=(
            pltpu.VMEM((r, d), F32),
            pltpu.VMEM((r, d), F32),
            pltpu.VMEM((halves, 1, r // halves), F32),
            pltpu.VMEM((1, t), F32),
        ),
        in_specs=[pl.BlockSpec(memory_space=pl.ANY)] * 4,
        out_specs=(vmem,) * 4,
        scratch_shapes=[
            pltpu.VMEM((r, d), F32),
            pltpu.VMEM((r, d), F32),
            pltpu.VMEM((logits.shape[0] // r, 1, r), F32),
            pltpu.VMEM((SQUARE, t, 2 * d), BF16),
            pltpu.VMEM((n_ca, r, 2 * d), BF16),
            pltpu.VMEM((n_ca, 1, r), F32),
            pltpu.VMEM((n_ca, r, 128), F32),
            pltpu.VMEM((n_ca, SQUARE, r, t), F32),
            pltpu.VMEM((n_ca, PIECES, SQUARE, 1, t // PIECES), F32),
            pltpu.VMEM((n_ca, PIECES, SQUARE, 1, t // PIECES), F32),
            pltpu.VMEM((PIECES, SQUARE, 1, t // PIECES), F32),
            pltpu.VMEM((PIECES, SQUARE, 1, t // PIECES), F32),
            pltpu.VMEM((n, PIECES, SQUARE, 1, t // PIECES), F32),
            pltpu.VMEM((n_ca, r, 2 * d), F32),
            pltpu.VMEM((r // halves, 128), F32),
            pltpu.VMEM((n_ca, halves, 1, r // halves), F32),
            pltpu.VMEM((n_ca, r, 2 * d), BF16),
            pltpu.VMEM((n_ca, halves, 1, r // halves), F32),
            pltpu.VMEM((n_ca + 1, r, 2 * d), BF16),
            pltpu.VMEM((n_ca + 1, halves, 1, r // halves), F32),
            dma((4,)),
            dma((6, PIECES)),
            dma((6, PIECES)),
            line, line, short, short,
            dma((n, PIECES)),
            dma((n, PIECES)),
            dma((n_ca, halves)),
            dma((n_ca + 1, halves)),
            dma((n_ca, halves)),
            dma((n_ca + 1, halves)),
        ],
        compiler_params=pltpu.CompilerParams(
            collective_id=0, has_side_effects=True, vmem_limit_bytes=VMEM_LIMIT
        ),
        name="em",
    )(images, means, precisions, logits.reshape(-1, 1, r))


def finish_kernel(total, first_ref, second_ref, den_ref, like_ref, nm_ref, nv_ref, nw_ref, ll_ref):
    halves, _, rh = den_ref.shape
    for h in range(halves):
        rows = slice(h * rh, (h + 1) * rh)
        den = den_ref[h]
        inv = 1.0 / jnp.broadcast_to(den, (128, rh)).T[:, :1]
        mean = first_ref[rows] * inv
        nm_ref[rows] = mean
        nv_ref[rows] = second_ref[rows] * inv - mean * mean
        nw_ref[h] = jnp.log(den) - jnp.log(jnp.float32(total))
    ll_ref[...] = like_ref[...]


def finish(total, first, second, den, like):
    vmem = pl.BlockSpec(memory_space=pltpu.VMEM)
    return pl.pallas_call(
        functools.partial(finish_kernel, total),
        out_shape=tuple(jax.ShapeDtypeStruct(x.shape, F32) for x in (first, second, den, like)),
        in_specs=[vmem] * 4,
        out_specs=(vmem,) * 4,
        name="finish",
    )(*(pltpu.with_memory_space_constraint(x, pltpu.VMEM) for x in (first, second, den, like)))


def body(n_ca, n_mp, images, means, precisions, logits):
    t, d = images.shape
    r = means.shape[0]
    total = float(t * n_ca * SQUARE + logits.shape[0])
    outs = em(images, means, precisions, logits, n_ca, n_mp)
    new_means, new_variances, new_log_weights, like = finish(total, *outs)
    return (new_means, new_variances, new_log_weights.reshape(r), like[0])


def solution(mesh):
    n_dp, n_mp = mesh.shape["dp"], mesh.shape["mp"]
    n_ca = n_dp // SQUARE
    split = Mesh(mesh.devices.reshape(n_ca, SQUARE, n_mp), ("ca", "ib", "mp"))
    dp = ("ca", "ib")
    comp = ("mp", "ca", "ib")
    return jax.shard_map(
        functools.partial(body, n_ca, n_mp),
        mesh=split,
        in_specs=(P(dp, None), P(comp, None), P(comp, None), P()),
        out_specs=(P(comp, None), P(comp, None), P(comp), P(dp)),
        check_vma=False,
    )
```
